256 devices in a mesh: frame: 8 (over x, y_lo), pos: 32 (over z, y_hi, core).
Axes of the slice: x: 4, y: 4 (y_hi: 2, y_lo: 2; y = y_hi * 2 + y_lo), z: 8, core: 2. Of those that a mesh axis runs over, the one named last changes fastest.
Arguments:
- frames_in: bfloat16 [512, 256, 512], P('frame', 'pos'), may hold values from -40 to 40
- attn_gain: float32 [512], replicated, may hold values from 0.5 to 1.5
- w_query: bfloat16 [512, 512], replicated, may hold values from -4 to 4
- w_key: bfloat16 [512, 512], replicated, may hold values from -4 to 4
- w_value: bfloat16 [512, 512], replicated, may hold values from -0.25 to 0.25
- w_output: bfloat16 [512, 512], replicated, may hold values from -0.25 to 0.25
- moe_gain: float32 [512], replicated, may hold values from 0.5 to 1.5
- dispatch_keys: bfloat16 [512, 1024], replicated, may hold values from -10 to 10
- w_in: bfloat16 [32, 512, 1024], P('pos'), may hold values from -0.25 to 0.25
- w_out: bfloat16 [32, 1024, 512], P('pos'), may hold values from -0.125 to 0.125
Outputs:
- frames_out: bfloat16 [512, 256, 512], P('frame', 'pos')
The draws below stay inside these ranges and needn't reach their ends.
All inputs are finite; a program needn't handle non-finite values.
Results may differ from the reference program's by a relative error of at most 0.0052.
Values may be sent and summed in bfloat16 or wider, within the bound.
No kernel may reach another device: no remote copies, remote signals or barrier semaphores. Data moves between devices by JAX's collectives and lax.ppermute only.
A program may use at most 64 MiB of HBM per device.

```python
import jax
import jax.numpy as jnp
from jax import lax

FR_DEV = 64
POSITIONS = 256
D = 512
HEADS = 8
EXPERTS = 16
SLOTS = 64
EXPERT_FF = 2048
SPLITS = 2
N_FRAME = 8


def draw_frames_in(key, part):
    array_shape = (FR_DEV * N_FRAME, POSITIONS, D)
    drawn = jax.random.normal(jax.random.fold_in(key, 1), array_shape, jnp.float32)
    return jnp.clip(drawn, -40.0, 40.0).astype(jnp.bfloat16)


def projection_draw(key, salt):
    baseline = jax.random.normal(jax.random.fold_in(key, salt), (D, D), jnp.float32) / jnp.sqrt(float(D))
    return jnp.clip(baseline, -4.0, 4.0).astype(jnp.bfloat16)


def draw_w_query(key, part):
    return projection_draw(key, 11)


def draw_w_key(key, part):
    return projection_draw(key, 12)


def draw_dispatch_keys(key, part):
    columns = EXPERTS * SLOTS
    baseline = jax.random.normal(jax.random.fold_in(key, 21), (D, columns), jnp.float32) / jnp.sqrt(float(D))
    return jnp.clip(baseline, -10.0, 10.0).astype(jnp.bfloat16)


def block_scale(key, extent, split, low, high):
    factor_of = 1.0
    for position, shards_of in split:
        draws = jax.random.uniform(jax.random.fold_in(jax.random.fold_in(key, 6), position), (shards_of,), jnp.float32, low / len(split), high / len(split))
        factor_of = factor_of * jnp.repeat(jnp.exp(draws), extent[position] // shards_of).reshape((-1,) + (1,) * (len(extent) - 1 - position))
    return factor_of


def normal_values(own_key, extent, deviation, limit, split=(), kind=jnp.bfloat16):
    factor_of = block_scale(own_key, extent, split, -0.22, 0.18) if split else 1.0
    array = jax.random.normal(own_key, extent, jnp.float32) * deviation * factor_of
    return jnp.minimum(jnp.maximum(array, -limit), limit).astype(kind)


def setup_inputs(seed: int = 0) -> dict:
    key_of = jax.random.split(jax.random.key(seed), 11)
    return {
        "frames_in": draw_frames_in(jax.random.fold_in(key_of[10], 71), 0),
        "attn_gain": jnp.clip(1.0 + 0.1 * jax.random.normal(key_of[1], (D,), jnp.float32), 0.5, 1.5),
        "w_query": draw_w_query(jax.random.fold_in(key_of[10], 71), 0),
        "w_key": draw_w_key(jax.random.fold_in(key_of[10], 71), 0),
        "w_value": normal_values(key_of[4], (D, D), D ** -0.5, 0.25),
        "w_output": normal_values(key_of[5], (D, D), D ** -0.5, 0.25),
        "moe_gain": jnp.clip(1.0 + 0.1 * jax.random.normal(key_of[6], (D,), jnp.float32), 0.5, 1.5),
        "dispatch_keys": draw_dispatch_keys(jax.random.fold_in(key_of[10], 71), 0),
        "w_in": normal_values(key_of[8], (EXPERTS * SPLITS, D, EXPERT_FF // SPLITS), D ** -0.5, 0.25, ((0, 32),)),
        "w_out": normal_values(key_of[9], (EXPERTS * SPLITS, EXPERT_FF // SPLITS, D), EXPERT_FF ** -0.5, 0.125, ((0, 32),)),
    }


EPS = 1e-06
LOGIT_SCALE = 3.0
MASKED = -1e+30

def rms_scale(values_in, gain):
    values_in = values_in.astype(jnp.float32)
    mean_sq = lax.optimization_barrier(jnp.mean(values_in * values_in, axis=-1, keepdims=True))
    return values_in * lax.rsqrt(mean_sq + EPS) * gain.astype(jnp.float32)

def project(rows_in, weights):
    return jnp.dot(rows_in, weights, preferred_element_type=jnp.float32).astype(jnp.bfloat16)

def softmax_rows(scores, axis_index):
    largest = lax.optimization_barrier(jnp.max(scores, axis=axis_index, keepdims=True))
    weights = jnp.exp(scores - largest)
    return (weights / lax.optimization_barrier(jnp.sum(weights, axis=axis_index, keepdims=True))).astype(jnp.bfloat16)

def reference(frames_in, attn_gain, w_query, w_key, w_value, w_output, moe_gain, dispatch_keys, w_in, w_out):
    frame_count, pos_count, features = frames_in.shape
    head_dim = features // HEADS
    score_scale = head_dim ** (-0.5)
    normed = rms_scale(frames_in, attn_gain).astype(jnp.bfloat16).reshape(frame_count * pos_count, features)
    shaped = (frame_count, pos_count, HEADS, head_dim)
    queries = project(normed, w_query).reshape(shaped).transpose(1, 0, 2, 3)
    keys_block = project(normed, w_key).reshape(shaped).transpose(1, 0, 2, 3)
    values_block = project(normed, w_value).reshape(shaped).transpose(1, 0, 2, 3)
    causal = jnp.arange(frame_count)[:, None] >= jnp.arange(frame_count)[None, :]

    def per_position(triple):
        queries_pos, keys_pos, values_pos = triple
        scores = jnp.einsum('fhd,ghd->hfg', queries_pos.astype(jnp.float32), keys_pos.astype(jnp.float32)) * score_scale
        scores = jnp.where(causal[None], scores, MASKED)
        attention = softmax_rows(scores, 2)
        return jnp.einsum('hfg,ghd->fhd', attention.astype(jnp.float32), values_pos.astype(jnp.float32)).astype(jnp.bfloat16)
    mixed_heads = lax.map(per_position, (queries, keys_block, values_block))
    mixed_heads = mixed_heads.transpose(1, 0, 2, 3).reshape(frame_count * pos_count, features)
    residual = (frames_in.reshape(frame_count * pos_count, features).astype(jnp.float32) + jnp.dot(mixed_heads, w_output, preferred_element_type=jnp.float32)).astype(jnp.bfloat16)
    moe_input = rms_scale(residual, moe_gain).astype(jnp.bfloat16)
    blocks = moe_input.reshape(frame_count // FR_DEV, FR_DEV * pos_count, features)
    splits = w_in.shape[0] // EXPERTS

    def per_block(block_rows):
        logits = LOGIT_SCALE * jnp.dot(block_rows, dispatch_keys, preferred_element_type=jnp.float32)
        dispatch = softmax_rows(logits, 0)
        slot_in = lax.dot_general(dispatch, block_rows, (((0,), (0,)), ((), ())), preferred_element_type=jnp.float32).astype(jnp.bfloat16)
        slot_in = jnp.repeat(slot_in.reshape(EXPERTS, SLOTS, features), splits, axis=0)
        hidden = jax.nn.gelu(jnp.einsum('esd,edh->esh', slot_in.astype(jnp.float32), w_in.astype(jnp.float32))).astype(jnp.bfloat16)
        partial_out = jnp.einsum('esh,ehd->esd', hidden.astype(jnp.float32), w_out.astype(jnp.float32)).astype(jnp.bfloat16)
        outputs = lax.optimization_barrier(jnp.sum(partial_out.astype(jnp.float32).reshape(EXPERTS, splits, SLOTS, features), axis=1))
        outputs = outputs.astype(jnp.bfloat16).reshape(EXPERTS * SLOTS, features)
        combine = softmax_rows(logits, 1)
        return jnp.dot(combine, outputs, preferred_element_type=jnp.float32)
    moe_out = lax.map(per_block, blocks).reshape(frame_count * pos_count, features)
    frames_out = (residual.astype(jnp.float32) + moe_out).astype(jnp.bfloat16)
    return frames_out.reshape(frame_count, pos_count, features)
```

```python
import jax
import jax.numpy as jnp
from jax import lax
from jax.experimental import pallas as pl
from jax.experimental.pallas import tpu as pltpu
from jax.sharding import PartitionSpec as P

HEADS = 8
EXPERTS = 16
SLOTS = 64

EPS = 1e-06
LOGIT_SCALE = 3.0
MASKED = -1e30
LOG2E = 1.4426950408889634

F32 = jnp.float32
BF16 = jnp.bfloat16
VMEM = pl.BlockSpec(memory_space=pltpu.VMEM)
STAT_ROWS = 8


def nn(a, b):
    return lax.dot_general(a, b, (((1,), (0,)), ((), ())), preferred_element_type=F32)


def nt(a, b):
    return lax.dot_general(a, b, (((1,), (1,)), ((), ())), preferred_element_type=F32)


def call(kernel, out_shape, args, scratch=(), flops=1 << 20, transcendentals=0):
    single = isinstance(out_shape, jax.ShapeDtypeStruct)
    outs = (out_shape,) if single else tuple(out_shape)
    moved = sum(a.size * a.dtype.itemsize for a in (*args, *outs))
    return pl.pallas_call(
        kernel,
        out_shape=out_shape,
        in_specs=[VMEM] * len(args),
        out_specs=VMEM if single else tuple([VMEM] * len(outs)),
        scratch_shapes=list(scratch),
        cost_estimate=pl.CostEstimate(
            flops=flops, bytes_accessed=moved, transcendentals=transcendentals
        ),
    )(*args)


def one_hot(rows, outer, inner):
    row = lax.broadcasted_iota(jnp.int32, (rows, rows), 0)
    col = lax.broadcasted_iota(jnp.int32, (rows, rows), 1)
    source = (row & (inner - 1)) * outer + lax.shift_right_logical(row, inner.bit_length() - 1)
    return jnp.where(col == source, 1.0, 0.0).astype(BF16)


def by_position_kernel(frames, positions, x_ref, o_ref):
    rows = frames * positions
    o_ref[...] = nn(one_hot(rows, positions, frames), x_ref[...]).astype(BF16)


def rms(rows, gain):
    mean_sq = jnp.mean(rows * rows, axis=-1, keepdims=True)
    return (rows * lax.rsqrt(mean_sq + EPS) * gain).astype(BF16)


def attention_kernel(x_ref, gain_ref, wq_ref, wk_ref, wv_ref, o_ref, n_s, q_s, k_s, v_s):
    frames, features = x_ref.shape
    n_s[...] = rms(x_ref[...].astype(F32), gain_ref[...])
    q_s[...] = nn(n_s[...], wq_ref[...]).astype(BF16)
    k_s[...] = nn(n_s[...], wk_ref[...]).astype(BF16)
    v_s[...] = nn(n_s[...], wv_ref[...]).astype(BF16)
    head_dim = features // HEADS
    scale = head_dim ** (-0.5) * LOG2E
    block = 256
    row = lax.broadcasted_iota(jnp.int32, (block, block), 0)
    col = lax.broadcasted_iota(jnp.int32, (block, block), 1)
    causal = row >= col
    low = lax.broadcasted_iota(jnp.int32, (1, 128), 1) < head_dim
    for pair in range(features // 128):
        lanes = slice(pair * 128, pair * 128 + 128)
        for start in range(0, frames, block):
            count = start + block
            mixed = []
            for mine in (low, jnp.logical_not(low)):
                q = jnp.where(mine, q_s[start:count, lanes], jnp.zeros((), BF16))
                t = nt(q, k_s[:count, lanes]) * scale
                last = jnp.where(causal, t[:, start:], MASKED)
                t = last if start == 0 else jnp.concatenate([t[:, :start], last], axis=1)
                weights = jnp.exp2(t - jnp.max(t, axis=1, keepdims=True)).astype(BF16)
                v = jnp.where(mine, v_s[:count, lanes], jnp.ones((), BF16))
                both = nn(weights, v)
                mixed.append(both / pltpu.roll(both, head_dim, 1))
            o_ref[start:count, lanes] = jnp.where(low, mixed[0], mixed[1]).astype(BF16)


def residual_kernel(mixed_ref, x_ref, wo_ref, gain_ref, r_ref, m_ref):
    r = (x_ref[...].astype(F32) + nn(mixed_ref[...], wo_ref[...])).astype(BF16)
    r_ref[...] = r
    m_ref[...] = rms(r.astype(F32), gain_ref[...])


def combine_kernel(m_ref, keys_ref, c_ref):
    rows = 128
    for start in range(0, m_ref.shape[0], rows):
        part = slice(start, start + rows)
        t = nn(m_ref[part, :], keys_ref[...]) * (LOGIT_SCALE * LOG2E)
        w = jnp.exp2(t - jnp.max(t, axis=1, keepdims=True))
        c_ref[part, :] = (w / jnp.sum(w, axis=1, keepdims=True)).astype(BF16)


def dispatch_kernel(m_ref, other_ref, keys_ref, o_ref, all_s):
    tokens, features = m_ref.shape
    all_s[:tokens, :] = m_ref[...]
    all_s[tokens:, :] = other_ref[...]
    half = SLOTS // 2
    for start in range(0, keys_ref.shape[0], 128):
        t = nt(keys_ref[start : start + 128, :], all_s[...]) * (LOGIT_SCALE * LOG2E)
        largest = jnp.max(t, axis=1, keepdims=True)
        w = jnp.exp2(t - largest)
        total = jnp.sum(w, axis=1, keepdims=True)
        sums = (nn(w.astype(BF16), all_s[...]) / total).astype(BF16)
        lse = jnp.broadcast_to(largest + jnp.log2(total), (128, 128)).T[:STAT_ROWS, :]
        high = lse.astype(BF16).astype(F32)
        middle = (lse - high).astype(BF16).astype(F32)
        rest = lse - high - middle
        line = lax.broadcasted_iota(jnp.int32, lse.shape, 0)
        stats = jnp.where(
            line == 0, high, jnp.where(line == 1, middle, jnp.where(line == 2, rest, 0.0))
        ).astype(BF16)
        for k in range(128 // half):
            expert = start // half + k
            for j in range(features // 128):
                o_ref[expert, j * half : (j + 1) * half, :] = sums[
                    k * half : (k + 1) * half, j * 128 : (j + 1) * 128
                ]
            o_ref[expert, features // 128 * half :, :] = stats


def merge_kernel(got_ref, o_ref, w_s):
    chips = got_ref.shape[0]
    half = SLOTS // 2
    tall = o_ref.shape[1] // 128 * half
    lse = jnp.concatenate(
        [
            jnp.sum(got_ref[s, tall:, :].astype(F32), axis=0, keepdims=True)
            for s in range(chips)
        ],
        axis=0,
    )
    w = jnp.exp2(lse - jnp.max(lse, axis=0, keepdims=True))
    w = w / jnp.sum(w, axis=0, keepdims=True)
    w_s[...] = jnp.concatenate([w, jnp.zeros((128 - chips, 128), F32)], axis=0).T
    place = lax.rem(lax.axis_index("pos") // 2, 128 // half)
    mine = w_s[pl.ds(pl.multiple_of(place * half, half), half), :]
    for j in range(o_ref.shape[1] // 128):
        total = jnp.zeros((half, 128), F32)
        for s in range(chips):
            total += mine[:, s : s + 1] * got_ref[s, j * half : (j + 1) * half, :].astype(F32)
        o_ref[:, j * 128 : (j + 1) * 128] = total.astype(BF16)


def expert_kernel(own_ref, other_ref, w_in_ref, w_out_ref, own_out, other_out):
    half = own_ref.shape[0]
    rows = jnp.concatenate([own_ref[...], other_ref[...]], axis=0)
    hidden = jax.nn.gelu(nn(rows, w_in_ref[...])).astype(BF16)
    out = nn(hidden, w_out_ref[...]).astype(BF16)
    own_out[...] = out[:half, :]
    other_out[...] = out[half:, :]


def output_kernel(frames, positions, r_ref, c_ref, own_ref, other_ref, o_ref, all_s):
    half = SLOTS // 2
    core = lax.rem(lax.axis_index("pos"), 2)
    for e in range(EXPERTS):
        part = slice(e * half, (e + 1) * half)
        at = pl.multiple_of(e * SLOTS + core * half, half)
        all_s[pl.ds(at, half), :] = own_ref[part, :]
        at = pl.multiple_of(e * SLOTS + (1 - core) * half, half)
        all_s[pl.ds(at, half), :] = other_ref[part, :]
    out = (r_ref[...].astype(F32) + nn(c_ref[...], all_s[...])).astype(BF16)
    o_ref[...] = nn(one_hot(frames * positions, frames, positions), out).astype(BF16)


def from_other_core(block):
    return lax.ppermute(block, "pos", [(k, k ^ 1) for k in range(lax.axis_size("pos"))])


def local(
    frames_in, attn_gain, w_query, w_key, w_value, w_output, moe_gain, dispatch_keys, w_in, w_out
):
    frame_count, pos_count, features = frames_in.shape
    tokens = frame_count * pos_count
    chips = lax.axis_size("pos") // 2
    half = SLOTS // 2
    by_core = [[2 * chip + core for chip in range(chips)] for core in range(2)]
    wide = jax.ShapeDtypeStruct((tokens, features), BF16)

    def by_position(x_ref, o_ref):
        by_position_kernel(frame_count, pos_count, x_ref, o_ref)

    def output(*refs):
        output_kernel(frame_count, pos_count, *refs)

    x = call(by_position, wide, (frames_in.reshape(tokens, features),), flops=2 * tokens**2 * features)
    spread = lax.all_to_all(
        x.reshape(pos_count, frame_count, features), "frame", split_axis=0, concat_axis=0, tiled=True
    )
    core = lax.rem(lax.axis_index("pos"), 2)
    by_half = dispatch_keys.T.reshape(EXPERTS, 2, half, features)
    half_keys = lax.dynamic_index_in_dim(by_half, core, 1, keepdims=False).reshape(-1, features)

    mixed = call(
        attention_kernel,
        wide,
        (spread.reshape(tokens, features), attn_gain.reshape(1, -1), w_query, w_key, w_value),
        scratch=[pltpu.VMEM((tokens, features), BF16)] * 4,
        flops=14 * tokens**2 * features,
        transcendentals=HEADS * tokens**2,
    )
    mixed = lax.all_to_all(
        mixed.reshape(pos_count, frame_count, features),
        "frame",
        split_axis=0,
        concat_axis=0,
        tiled=True,
    )
    residual, moe_input = call(
        residual_kernel,
        (wide, wide),
        (mixed.reshape(tokens, features), x, w_output, moe_gain.reshape(1, -1)),
        flops=2 * tokens**2 * features,
    )
    other_input = from_other_core(moe_input)
    combine = call(
        combine_kernel,
        jax.ShapeDtypeStruct((tokens, EXPERTS * SLOTS), BF16),
        (moe_input, dispatch_keys),
        flops=4 * tokens**2 * features,
        transcendentals=2 * tokens**2,
    )
    sums = call(
        dispatch_kernel,
        jax.ShapeDtypeStruct((chips, features // 128 * half + STAT_ROWS, 128), BF16),
        (moe_input, other_input, half_keys),
        scratch=[pltpu.VMEM((2 * tokens, features), BF16)],
        flops=8 * tokens**2 * features,
        transcendentals=2 * tokens**2,
    )
    sums = lax.all_to_all(
        sums, "pos", split_axis=0, concat_axis=0, tiled=True, axis_index_groups=by_core
    )
    narrow = jax.ShapeDtypeStruct((half, features), BF16)
    slot_in = call(merge_kernel, narrow, (sums,), scratch=[pltpu.VMEM((128, 128), F32)])
    other_slots = from_other_core(slot_in)
    own_part, other_part = call(
        expert_kernel,
        (narrow, narrow),
        (slot_in, other_slots, w_in[0], w_out[0]),
        flops=8 * SLOTS * features**2,
    )
    outputs = (own_part.astype(F32) + from_other_core(other_part).astype(F32)).astype(BF16)
    own_half = lax.all_to_all(
        jnp.broadcast_to(outputs, (chips, *outputs.shape)),
        "pos",
        split_axis=0,
        concat_axis=0,
        tiled=True,
        axis_index_groups=by_core,
    ).reshape(-1, features)
    other_half = from_other_core(own_half)
    out = call(
        output,
        wide,
        (residual, combine, own_half, other_half),
        scratch=[pltpu.VMEM((EXPERTS * SLOTS, features), BF16)],
        flops=6 * tokens**2 * features,
    )
    return out.reshape(frame_count, pos_count, features)


def solution(mesh):
    in_specs = (
        P("frame", "pos", None),
        P(),
        P(),
        P(),
        P(),
        P(),
        P(),
        P(),
        P("pos", None, None),
        P("pos", None, None),
    )
    out_specs = P("frame", "pos", None)
    return jax.shard_map(local, mesh=mesh, in_specs=in_specs, out_specs=out_specs, check_vma=False)
```

```python
import jax
import jax.numpy as jnp
from jax import lax
from jax.experimental import pallas as pl
from jax.experimental.pallas import tpu as pltpu
from jax.sharding import PartitionSpec as P


HEADS = 8
EXPERTS = 16
SLOTS = 64

EPS = 1e-06
LOGIT_SCALE = 3.0
MASKED = -1e30
LOG2E = 1.4426950408889634

F32 = jnp.float32
BF16 = jnp.bfloat16
VMEM = pl.BlockSpec(memory_space=pltpu.VMEM)
STAT_ROWS = 8


def nn(a, b):
    return lax.dot_general(a, b, (((1,), (0,)), ((), ())), preferred_element_type=F32)


def nt(a, b):
    return lax.dot_general(a, b, (((1,), (1,)), ((), ())), preferred_element_type=F32)


def call(kernel, out_shape, args, scratch=(), flops=1 << 20, transcendentals=0, left=0):
    single = isinstance(out_shape, jax.ShapeDtypeStruct)
    outs = (out_shape,) if single else tuple(out_shape)
    moved = sum(a.size * a.dtype.itemsize for a in (*args, *outs))
    return pl.pallas_call(
        kernel,
        out_shape=out_shape,
        in_specs=[VMEM] * (len(args) - left) + [pl.BlockSpec(memory_space=pltpu.HBM)] * left,
        out_specs=VMEM if single else tuple([VMEM] * len(outs)),
        scratch_shapes=list(scratch),
        compiler_params=pltpu.CompilerParams(vmem_limit_bytes=16 << 20),
        cost_estimate=pl.CostEstimate(
            flops=flops, bytes_accessed=moved, transcendentals=transcendentals
        ),
    )(*args)


def one_hot(rows, outer, inner):
    row = lax.broadcasted_iota(jnp.int32, (rows, rows), 0)
    col = lax.broadcasted_iota(jnp.int32, (rows, rows), 1)
    source = (row & (inner - 1)) * outer + lax.shift_right_logical(row, inner.bit_length() - 1)
    return jnp.where(col == source, 1.0, 0.0).astype(BF16)


def by_position_kernel(
    frames, positions, x_ref, gain_ref, moe_ref, o_ref, gain_out, moe_out, back_ref, x_s, sems
):
    copies = (
        pltpu.make_async_copy(x_ref, x_s, sems.at[0]),
        pltpu.make_async_copy(gain_ref, gain_out, sems.at[1]),
        pltpu.make_async_copy(moe_ref, moe_out, sems.at[2]),
    )
    for copy in copies:
        copy.start()
    order = one_hot(frames * positions, positions, frames)
    back_ref[...] = one_hot(frames * positions, frames, positions)
    for copy in copies:
        copy.wait()
    o_ref[...] = nn(order, x_s[...]).astype(BF16)


def rms(rows, gain):
    mean_sq = jnp.mean(rows * rows, axis=-1, keepdims=True)
    return (rows * lax.rsqrt(mean_sq + EPS) * gain).astype(BF16)


def attention_kernel(x_ref, gain_ref, wq_ref, wk_ref, wv_ref, o_ref, n_s, q_s, k_s, v_s):
    frames, features = x_ref.shape
    n_s[...] = rms(x_ref[...].astype(F32), gain_ref[...])
    q_s[...] = nn(n_s[...], wq_ref[...]).astype(BF16)
    k_s[...] = nn(n_s[...], wk_ref[...]).astype(BF16)
    v_s[...] = nn(n_s[...], wv_ref[...]).astype(BF16)
    head_dim = features // HEADS
    scale = head_dim ** (-0.5) * LOG2E
    block = 256
    row = lax.broadcasted_iota(jnp.int32, (block, block), 0)
    col = lax.broadcasted_iota(jnp.int32, (block, block), 1)
    causal = row >= col
    low = lax.broadcasted_iota(jnp.int32, (1, 128), 1) < head_dim
    for pair in range(features // 128):
        lanes = slice(pair * 128, pair * 128 + 128)
        for start in range(0, frames, block):
            count = start + block
            mixed = []
            for mine in (low, jnp.logical_not(low)):
                q = jnp.where(mine, q_s[start:count, lanes], jnp.zeros((), BF16))
                t = nt(q, k_s[:count, lanes]) * scale
                last = jnp.where(causal, t[:, start:], MASKED)
                t = last if start == 0 else jnp.concatenate([t[:, :start], last], axis=1)
                weights = jnp.exp2(t - jnp.max(t, axis=1, keepdims=True)).astype(BF16)
                v = jnp.where(mine, v_s[:count, lanes], jnp.ones((), BF16))
                both = nn(weights, v)
                mixed.append(both / pltpu.roll(both, head_dim, 1))
            o_ref[start:count, lanes] = jnp.where(low, mixed[0], mixed[1]).astype(BF16)


def residual_kernel(mixed_ref, x_ref, wo_ref, gain_ref, r_ref, m_ref):
    r = (x_ref[...].astype(F32) + nn(mixed_ref[...], wo_ref[...])).astype(BF16)
    r_ref[...] = r
    m_ref[...] = rms(r.astype(F32), gain_ref[...])


def keys_kernel(keys_ref, slots_ref):
    half = SLOTS // 2
    core = lax.rem(lax.axis_index("pos"), 2)
    row = lax.broadcasted_iota(jnp.int32, (128, 256), 0)
    col = lax.broadcasted_iota(jnp.int32, (128, 256), 1)
    first = (row // half) * SLOTS + (row & (half - 1))
    count = keys_ref.shape[1] // 2
    for turn in range(2):
        taken = core if turn == 0 else 1 - core
        pick = jnp.where(col == first + taken * half, 1.0, 0.0).astype(BF16)
        for k in range(count // 128):
            at = turn * count + k * 128
            keys = nt(pick, keys_ref[:, 256 * k : 256 * k + 256])
            slots_ref[at : at + 128, :] = keys.astype(BF16)


def combine_kernel(m_ref, slots_ref, c_ref):
    rows = 256
    for start in range(0, m_ref.shape[0], rows):
        part = slice(start, start + rows)
        t = nt(m_ref[part, :], slots_ref[...]) * (LOGIT_SCALE * LOG2E)
        w = jnp.exp2(t - jnp.max(t, axis=1, keepdims=True))
        c_ref[part, :] = (w / jnp.sum(w, axis=1, keepdims=True)).astype(BF16)


def dispatch_kernel(m_ref, other_ref, keys_ref, o_ref, all_s):
    tokens, features = m_ref.shape
    all_s[:tokens, :] = m_ref[...]
    all_s[tokens:, :] = other_ref[...]
    half = SLOTS // 2
    rows = 256
    for start in range(0, keys_ref.shape[0] // 2, rows):
        t = nt(keys_ref[start : start + rows, :], all_s[...]) * (LOGIT_SCALE * LOG2E)
        largest = jnp.max(t, axis=1, keepdims=True)
        w = jnp.exp2(t - largest)
        total = jnp.sum(w, axis=1, keepdims=True)
        sums = (nn(w.astype(BF16), all_s[...]) / total).astype(BF16)
        for k in range(rows // half):
            expert = start // half + k
            for j in range(features // 128):
                o_ref[expert, j * half : (j + 1) * half, :] = sums[
                    k * half : (k + 1) * half, j * 128 : (j + 1) * 128
                ]
        column = largest + jnp.log2(total)
        for at in range(0, rows, 128):
            lse = jnp.broadcast_to(column[at : at + 128], (128, 128)).T[:STAT_ROWS, :]
            high = lse.astype(BF16).astype(F32)
            middle = (lse - high).astype(BF16).astype(F32)
            rest = lse - high - middle
            line = lax.broadcasted_iota(jnp.int32, lse.shape, 0)
            stats = jnp.where(
                line == 0, high, jnp.where(line == 1, middle, jnp.where(line == 2, rest, 0.0))
            ).astype(BF16)
            for k in range(128 // half):
                o_ref[(start + at) // half + k, features // 128 * half :, :] = stats


def expert_kernel(got_ref, w_in_ref, other_in_ref, w_out_ref, other_out_ref, o_ref, w_s):
    chips, half, features = o_ref.shape
    tall = features // 128 * half
    lse = jnp.concatenate(
        [
            jnp.sum(got_ref[s, tall:, :].astype(F32), axis=0, keepdims=True)
            for s in range(chips)
        ],
        axis=0,
    )
    w = jnp.exp2(lse - jnp.max(lse, axis=0, keepdims=True))
    w = w / jnp.sum(w, axis=0, keepdims=True)
    w_s[...] = jnp.concatenate([w, jnp.zeros((128 - chips, 128), F32)], axis=0).T
    place = lax.rem(lax.axis_index("pos") // 2, 128 // half)
    mine = w_s[pl.ds(pl.multiple_of(place * half, half), half), :]
    columns = []
    for j in range(features // 128):
        total = jnp.zeros((half, 128), F32)
        for s in range(chips):
            total += mine[:, s : s + 1] * got_ref[s, j * half : (j + 1) * half, :].astype(F32)
        columns.append(total.astype(BF16))
    slot_in = jnp.concatenate(columns, axis=1)
    out = jnp.zeros((half, features), F32)
    for first, second in ((w_in_ref, w_out_ref), (other_in_ref, other_out_ref)):
        hidden = jax.nn.gelu(nn(slot_in, first[...])).astype(BF16)
        out += nn(hidden, second[...]).astype(BF16).astype(F32)
    out = out.astype(BF16)
    for s in range(chips):
        o_ref[s] = out


def own_kernel(r_ref, c_ref, own_ref, o_ref):
    count = own_ref.shape[0]
    o_ref[...] = r_ref[...].astype(F32) + nn(c_ref[:, :count], own_ref[...])


def output_kernel(sum_ref, c_ref, other_ref, back_ref, o_ref):
    count = other_ref.shape[0]
    out = (sum_ref[...] + nn(c_ref[:, count:], other_ref[...])).astype(BF16)
    o_ref[...] = nn(back_ref[...], out).astype(BF16)


def from_other_core(block):
    return lax.ppermute(block, "pos", [(k, k ^ 1) for k in range(lax.axis_size("pos"))])


def local(
    frames_in, attn_gain, w_query, w_key, w_value, w_output, moe_gain, dispatch_keys, w_in, w_out
):
    frame_count, pos_count, features = frames_in.shape
    tokens = frame_count * pos_count
    chips = lax.axis_size("pos") // 2
    half = SLOTS // 2
    by_core = [[2 * chip + core for chip in range(chips)] for core in range(2)]
    wide = jax.ShapeDtypeStruct((tokens, features), BF16)

    def by_position(*refs):
        by_position_kernel(frame_count, pos_count, *refs)

    def over_frames(block):
        block = block.reshape(pos_count, frame_count, features)
        block = lax.all_to_all(block, "frame", split_axis=0, concat_axis=0, tiled=True)
        return block.reshape(tokens, features)

    def over_chips(blocks):
        return lax.all_to_all(
            blocks, "pos", split_axis=0, concat_axis=0, tiled=True, axis_index_groups=by_core
        )

    other_in = from_other_core(w_in[0])
    other_out = from_other_core(w_out[0])
    line = jax.ShapeDtypeStruct((1, features), F32)
    x, gain, gain_moe, back = call(
        by_position,
        (wide, line, line, jax.ShapeDtypeStruct((tokens, tokens), BF16)),
        (frames_in.reshape(tokens, features), attn_gain.reshape(1, -1), moe_gain.reshape(1, -1)),
        scratch=[pltpu.VMEM((tokens, features), BF16), pltpu.SemaphoreType.DMA((3,))],
        left=3,
        flops=2 * tokens**2 * features,
    )
    mixed = call(
        attention_kernel,
        wide,
        (over_frames(x), gain, w_query, w_key, w_value),
        scratch=[pltpu.VMEM((tokens, features), BF16)] * 4,
        flops=14 * tokens**2 * features,
        transcendentals=HEADS * tokens**2,
    )
    residual, moe_input = call(
        residual_kernel,
        (wide, wide),
        (over_frames(mixed), x, w_output, gain_moe),
        flops=2 * tokens**2 * features,
    )
    other_input = from_other_core(moe_input)
    slot_keys = call(
        keys_kernel,
        jax.ShapeDtypeStruct((EXPERTS * SLOTS, features), BF16),
        (dispatch_keys,),
        flops=512 * tokens * features,
    )
    sums = call(
        dispatch_kernel,
        jax.ShapeDtypeStruct((chips, features // 128 * half + STAT_ROWS, 128), BF16),
        (moe_input, other_input, slot_keys),
        scratch=[pltpu.VMEM((2 * tokens, features), BF16)],
        flops=8 * tokens**2 * features,
        transcendentals=2 * tokens**2,
    )
    outputs = call(
        expert_kernel,
        jax.ShapeDtypeStruct((chips, half, features), BF16),
        (over_chips(sums), w_in[0], other_in, w_out[0], other_out),
        scratch=[pltpu.VMEM((128, 128), F32)],
        flops=16 * SLOTS * features**2,
    )
    own_half = over_chips(outputs).reshape(-1, features)
    other_half = from_other_core(own_half)
    combine = call(
        combine_kernel,
        jax.ShapeDtypeStruct((tokens, EXPERTS * SLOTS), BF16),
        (moe_input, slot_keys),
        flops=4 * tokens**2 * features,
        transcendentals=2 * tokens**2,
    )
    own_sum = call(
        own_kernel,
        jax.ShapeDtypeStruct((tokens, features), F32),
        (residual, combine, own_half),
        flops=2 * tokens**2 * features,
    )
    out = call(
        output_kernel, wide, (own_sum, combine, other_half, back), flops=4 * tokens**2 * features
    )
    return out.reshape(frame_count, pos_count, features)


def solution(mesh):
    in_specs = (
        P("frame", "pos", None),
        P(),
        P(),
        P(),
        P(),
        P(),
        P(),
        P(),
        P("pos", None, None),
        P("pos", None, None),
    )
    out_specs = P("frame", "pos", None)

    return jax.shard_map(local, mesh=mesh, in_specs=in_specs, out_specs=out_specs, check_vma=False)
```

```python
import jax
import jax.numpy as jnp
from jax import lax
from jax.experimental import pallas as pl
from jax.experimental.pallas import tpu as pltpu
from jax.sharding import PartitionSpec as P


HEADS = 8
EXPERTS = 16
SLOTS = 64

EPS = 1e-06
LOGIT_SCALE = 3.0
MASKED = -1e30
LOG2E = 1.4426950408889634

F32 = jnp.float32
BF16 = jnp.bfloat16
VMEM = pl.BlockSpec(memory_space=pltpu.VMEM)
STAT_ROWS = 8
ORDER = tuple(2 * z + y for y in range(2) for z in range(8))


def nn(a, b):
    return lax.dot_general(a, b, (((1,), (0,)), ((), ())), preferred_element_type=F32)


def nt(a, b):
    return lax.dot_general(a, b, (((1,), (1,)), ((), ())), preferred_element_type=F32)


def call(kernel, out_shape, args, scratch=(), flops=1 << 20, transcendentals=0, left=0):
    single = isinstance(out_shape, jax.ShapeDtypeStruct)
    outs = (out_shape,) if single else tuple(out_shape)
    moved = sum(a.size * a.dtype.itemsize for a in (*args, *outs))
    return pl.pallas_call(
        kernel,
        out_shape=out_shape,
        in_specs=[VMEM] * (len(args) - left) + [pl.BlockSpec(memory_space=pltpu.HBM)] * left,
        out_specs=VMEM if single else tuple([VMEM] * len(outs)),
        scratch_shapes=list(scratch),
        compiler_params=pltpu.CompilerParams(vmem_limit_bytes=16 << 20),
        cost_estimate=pl.CostEstimate(
            flops=flops, bytes_accessed=moved, transcendentals=transcendentals
        ),
    )(*args)


def one_hot(rows, outer, inner):
    row = lax.broadcasted_iota(jnp.int32, (rows, rows), 0)
    col = lax.broadcasted_iota(jnp.int32, (rows, rows), 1)
    source = (row & (inner - 1)) * outer + lax.shift_right_logical(row, inner.bit_length() - 1)
    return jnp.where(col == source, 1.0, 0.0).astype(BF16)


def by_position_kernel(
    frames, positions, x_ref, gain_ref, moe_ref, o_ref, gain_out, moe_out, back_ref, x_s, sems
):
    copies = (
        pltpu.make_async_copy(x_ref, x_s, sems.at[0]),
        pltpu.make_async_copy(gain_ref, gain_out, sems.at[1]),
        pltpu.make_async_copy(moe_ref, moe_out, sems.at[2]),
    )
    for copy in copies:
        copy.start()
    order = one_hot(frames * positions, positions, frames)
    back_ref[...] = one_hot(frames * positions, frames, positions)
    for copy in copies:
        copy.wait()
    o_ref[...] = nn(order, x_s[...]).astype(BF16)


def rms(rows, gain):
    mean_sq = jnp.mean(rows * rows, axis=-1, keepdims=True)
    return (rows * lax.rsqrt(mean_sq + EPS) * gain).astype(BF16)


def attention_kernel(x_ref, gain_ref, wq_ref, wk_ref, wv_ref, o_ref, n_s, q_s, k_s, v_s, w_s):
    frames, features = x_ref.shape
    head_dim = features // HEADS
    n_s[...] = rms(x_ref[...].astype(F32), gain_ref[...])
    q_s[...] = (nn(n_s[...], wq_ref[...]) * (head_dim ** (-0.5) * LOG2E)).astype(BF16)
    k_s[...] = nn(n_s[...], wk_ref[...]).astype(BF16)
    v_s[...] = nn(n_s[...], wv_ref[...]).astype(BF16)
    half = frames // 2
    row = lax.broadcasted_iota(jnp.int32, (half, half), 0)
    col = lax.broadcasted_iota(jnp.int32, (half, half), 1)
    causal = row >= col
    low = lax.broadcasted_iota(jnp.int32, (1, 128), 1) < head_dim
    w_s[:half, half:] = jnp.zeros((half, half), BF16)
    for pair in range(features // 128):
        lanes = slice(pair * 128, pair * 128 + 128)
        mixed = []
        for mine in (low, jnp.logical_not(low)):
            q = jnp.where(mine, q_s[:, lanes], jnp.zeros((), BF16))
            t = nt(q, k_s[:, lanes])
            first = jnp.where(causal, t[:half, :half], MASKED)
            w = jnp.exp2(first - jnp.max(first, axis=1, keepdims=True))
            w_s[:half, :half] = w.astype(BF16)
            before = t[half:, :half]
            last = jnp.where(causal, t[half:, half:], MASKED)
            largest = jnp.maximum(
                jnp.max(before, axis=1, keepdims=True), jnp.max(last, axis=1, keepdims=True)
            )
            w_s[half:, :half] = jnp.exp2(before - largest).astype(BF16)
            w_s[half:, half:] = jnp.exp2(last - largest).astype(BF16)
            v = jnp.where(mine, v_s[:, lanes], jnp.ones((), BF16))
            mixed.append(nn(w_s[...], v))
        total = pltpu.roll(jnp.where(low, mixed[1], mixed[0]), head_dim, 1)
        o_ref[:, lanes] = (jnp.where(low, mixed[0], mixed[1]) / total).astype(BF16)


def residual_kernel(mixed_ref, x_ref, wo_ref, gain_ref, r_ref, m_ref):
    r = (x_ref[...].astype(F32) + nn(mixed_ref[...], wo_ref[...])).astype(BF16)
    r_ref[...] = r
    m_ref[...] = rms(r.astype(F32), gain_ref[...])


def keys_kernel(keys_ref, slots_ref):
    half = SLOTS // 2
    core = lax.rem(lax.axis_index("pos"), 2)
    row = lax.broadcasted_iota(jnp.int32, (128, 256), 0)
    col = lax.broadcasted_iota(jnp.int32, (128, 256), 1)
    first = (row // half) * SLOTS + (row & (half - 1))
    count = keys_ref.shape[1] // 2
    for turn in range(2):
        taken = core if turn == 0 else 1 - core
        pick = jnp.where(col == first + taken * half, 1.0, 0.0).astype(BF16)
        for k in range(count // 128):
            keys = nt(pick, keys_ref[:, 256 * k : 256 * k + 256]).astype(BF16)
            for i in range(128 // half):
                at = turn * count + half * ORDER.index(k * (128 // half) + i)
                slots_ref[at : at + half, :] = keys[i * half : (i + 1) * half, :]


def combine_kernel(m_ref, slots_ref, c_ref):
    rows = 256
    for start in range(0, m_ref.shape[0], rows):
        part = slice(start, start + rows)
        t = nt(m_ref[part, :], slots_ref[...]) * (LOGIT_SCALE * LOG2E)
        w = jnp.exp2(t - jnp.max(t, axis=1, keepdims=True))
        c_ref[part, :] = (w / jnp.sum(w, axis=1, keepdims=True)).astype(BF16)


def dispatch_kernel(m_ref, other_ref, keys_ref, o_ref, all_s):
    tokens, features = m_ref.shape
    all_s[:tokens, :] = m_ref[...]
    all_s[tokens:, :] = other_ref[...]
    half = SLOTS // 2
    rows = 256
    for start in range(0, keys_ref.shape[0] // 2, rows):
        t = nt(keys_ref[start : start + rows, :], all_s[...]) * (LOGIT_SCALE * LOG2E)
        largest = jnp.max(t, axis=1, keepdims=True)
        w = jnp.exp2(t - largest)
        total = jnp.sum(w, axis=1, keepdims=True)
        sums = (nn(w.astype(BF16), all_s[...]) / total).astype(BF16)
        for k in range(rows // half):
            expert = start // half + k
            for j in range(features // 128):
                o_ref[expert, j * half : (j + 1) * half, :] = sums[
                    k * half : (k + 1) * half, j * 128 : (j + 1) * 128
                ]
        column = largest + jnp.log2(total)
        for at in range(0, rows, 128):
            lse = jnp.broadcast_to(column[at : at + 128], (128, 128)).T[:STAT_ROWS, :]
            high = lse.astype(BF16).astype(F32)
            middle = (lse - high).astype(BF16).astype(F32)
            rest = lse - high - middle
            line = lax.broadcasted_iota(jnp.int32, lse.shape, 0)
            stats = jnp.where(
                line == 0, high, jnp.where(line == 1, middle, jnp.where(line == 2, rest, 0.0))
            ).astype(BF16)
            for k in range(128 // half):
                o_ref[(start + at) // half + k, features // 128 * half :, :] = stats


def expert_kernel(got_ref, w_in_ref, other_in_ref, w_out_ref, other_out_ref, o_ref, w_s):
    chips, half, features = o_ref.shape
    tall = features // 128 * half
    lse = jnp.concatenate(
        [
            jnp.sum(got_ref[s, tall:, :].astype(F32), axis=0, keepdims=True)
            for s in range(chips)
        ],
        axis=0,
    )
    w = jnp.exp2(lse - jnp.max(lse, axis=0, keepdims=True))
    w = w / jnp.sum(w, axis=0, keepdims=True)
    w_s[...] = jnp.concatenate([w, jnp.zeros((128 - chips, 128), F32)], axis=0).T
    chip = lax.axis_index("pos") // 2
    place = sum(jnp.where(chip == ORDER[k], k, 0) for k in range(chips))
    place = lax.rem(place, 128 // half)
    mine = w_s[pl.ds(pl.multiple_of(place * half, half), half), :]
    columns = []
    for j in range(features // 128):
        total = jnp.zeros((half, 128), F32)
        for s in range(chips):
            total += mine[:, s : s + 1] * got_ref[s, j * half : (j + 1) * half, :].astype(F32)
        columns.append(total.astype(BF16))
    slot_in = jnp.concatenate(columns, axis=1)
    out = jnp.zeros((half, features), F32)
    for first, second in ((w_in_ref, w_out_ref), (other_in_ref, other_out_ref)):
        hidden = jax.nn.gelu(nn(slot_in, first[...])).astype(BF16)
        out += nn(hidden, second[...]).astype(BF16).astype(F32)
    out = out.astype(BF16)
    for s in range(chips):
        o_ref[s] = out


def own_kernel(r_ref, c_ref, own_ref, o_ref):
    count = own_ref.shape[0]
    o_ref[...] = r_ref[...].astype(F32) + nn(c_ref[:, :count], own_ref[...])


def output_kernel(sum_ref, c_ref, other_ref, back_ref, o_ref):
    count = other_ref.shape[0]
    out = (sum_ref[...] + nn(c_ref[:, count:], other_ref[...])).astype(BF16)
    o_ref[...] = nn(back_ref[...], out).astype(BF16)


def from_other_core(block):
    return lax.ppermute(block, "pos", [(k, k ^ 1) for k in range(lax.axis_size("pos"))])


def local(
    frames_in, attn_gain, w_query, w_key, w_value, w_output, moe_gain, dispatch_keys, w_in, w_out
):
    frame_count, pos_count, features = frames_in.shape
    tokens = frame_count * pos_count
    chips = lax.axis_size("pos") // 2
    half = SLOTS // 2
    by_core = [[2 * chip + core for chip in ORDER] for core in range(2)]
    wide = jax.ShapeDtypeStruct((tokens, features), BF16)

    def by_position(*refs):
        by_position_kernel(frame_count, pos_count, *refs)

    def over_frames(block):
        block = block.reshape(pos_count, frame_count, features)
        block = lax.all_to_all(block, "frame", split_axis=0, concat_axis=0, tiled=True)
        return block.reshape(tokens, features)

    def over_chips(blocks):
        return lax.all_to_all(
            blocks, "pos", split_axis=0, concat_axis=0, tiled=True, axis_index_groups=by_core
        )

    other_in = from_other_core(w_in[0])
    other_out = from_other_core(w_out[0])
    line = jax.ShapeDtypeStruct((1, features), F32)
    x, gain, gain_moe, back = call(
        by_position,
        (wide, line, line, jax.ShapeDtypeStruct((tokens, tokens), BF16)),
        (frames_in.reshape(tokens, features), attn_gain.reshape(1, -1), moe_gain.reshape(1, -1)),
        scratch=[pltpu.VMEM((tokens, features), BF16), pltpu.SemaphoreType.DMA((3,))],
        left=3,
        flops=2 * tokens**2 * features,
    )
    mixed = call(
        attention_kernel,
        wide,
        (over_frames(x), gain, w_query, w_key, w_value),
        scratch=[pltpu.VMEM((tokens, features), BF16)] * 4 + [pltpu.VMEM((tokens, tokens), BF16)],
        flops=14 * tokens**2 * features,
        transcendentals=HEADS * tokens**2,
    )
    residual, moe_input = call(
        residual_kernel,
        (wide, wide),
        (over_frames(mixed), x, w_output, gain_moe),
        flops=2 * tokens**2 * features,
    )
    other_input = from_other_core(moe_input)
    slot_keys = call(
        keys_kernel,
        jax.ShapeDtypeStruct((EXPERTS * SLOTS, features), BF16),
        (dispatch_keys,),
        flops=512 * tokens * features,
    )
    sums = call(
        dispatch_kernel,
        jax.ShapeDtypeStruct((chips, features // 128 * half + STAT_ROWS, 128), BF16),
        (moe_input, other_input, slot_keys),
        scratch=[pltpu.VMEM((2 * tokens, features), BF16)],
        flops=8 * tokens**2 * features,
        transcendentals=2 * tokens**2,
    )
    outputs = call(
        expert_kernel,
        jax.ShapeDtypeStruct((chips, half, features), BF16),
        (over_chips(sums), w_in[0], other_in, w_out[0], other_out),
        scratch=[pltpu.VMEM((128, 128), F32)],
        flops=16 * SLOTS * features**2,
    )
    own_half = over_chips(outputs).reshape(-1, features)
    other_half = from_other_core(own_half)
    combine = call(
        combine_kernel,
        jax.ShapeDtypeStruct((tokens, EXPERTS * SLOTS), BF16),
        (moe_input, slot_keys),
        flops=4 * tokens**2 * features,
        transcendentals=2 * tokens**2,
    )
    own_sum = call(
        own_kernel,
        jax.ShapeDtypeStruct((tokens, features), F32),
        (residual, combine, own_half),
        flops=2 * tokens**2 * features,
    )
    out = call(
        output_kernel, wide, (own_sum, combine, other_half, back), flops=4 * tokens**2 * features
    )
    return out.reshape(frame_count, pos_count, features)


def solution(mesh):
    in_specs = (
        P("frame", "pos", None),
        P(),
        P(),
        P(),
        P(),
        P(),
        P(),
        P(),
        P("pos", None, None),
        P("pos", None, None),
    )
    out_specs = P("frame", "pos", None)

    return jax.shard_map(local, mesh=mesh, in_specs=in_specs, out_specs=out_specs, check_vma=False)
```

```python
import jax
import jax.numpy as jnp
from jax import lax
from jax.experimental import pallas as pl
from jax.experimental.pallas import tpu as pltpu
from jax.sharding import PartitionSpec as P


HEADS = 8
EXPERTS = 16
SLOTS = 64

EPS = 1e-06
LOGIT_SCALE = 3.0
MASKED = -1e30
LOG2E = 1.4426950408889634

F32 = jnp.float32
BF16 = jnp.bfloat16
VMEM = pl.BlockSpec(memory_space=pltpu.VMEM)
STAT_ROWS = 8
ORDER = (9, 11, 13, 15, 1, 3, 5, 7, 8, 10, 12, 14, 0, 2, 4, 6)


def nn(a, b):
    return lax.dot_general(a, b, (((1,), (0,)), ((), ())), preferred_element_type=F32)


def nt(a, b):
    return lax.dot_general(a, b, (((1,), (1,)), ((), ())), preferred_element_type=F32)


def call(kernel, out_shape, args, scratch=(), flops=1 << 20, transcendentals=0):
    single = isinstance(out_shape, jax.ShapeDtypeStruct)
    outs = (out_shape,) if single else tuple(out_shape)
    moved = sum(a.size * a.dtype.itemsize for a in (*args, *outs))
    return pl.pallas_call(
        kernel,
        out_shape=out_shape,
        in_specs=[VMEM] * len(args),
        out_specs=VMEM if single else tuple([VMEM] * len(outs)),
        scratch_shapes=list(scratch),
        compiler_params=pltpu.CompilerParams(vmem_limit_bytes=16 << 20),
        cost_estimate=pl.CostEstimate(
            flops=flops, bytes_accessed=moved, transcendentals=transcendentals
        ),
    )(*args)


def one_hot(rows, outer, inner):
    row = lax.broadcasted_iota(jnp.int32, (rows, rows), 0)
    col = lax.broadcasted_iota(jnp.int32, (rows, rows), 1)
    source = (row & (inner - 1)) * outer + lax.shift_right_logical(row, inner.bit_length() - 1)
    return jnp.where(col == source, 1.0, 0.0).astype(BF16)


def by_position_kernel(frames, positions, x_ref, gain_ref, moe_ref, o_ref, gain_out, moe_out):
    gain_out[...] = gain_ref[...]
    moe_out[...] = moe_ref[...]
    o_ref[...] = nn(one_hot(frames * positions, positions, frames), x_ref[...]).astype(BF16)


def rms(rows, gain):
    mean_sq = jnp.mean(rows * rows, axis=-1, keepdims=True)
    return (rows * lax.rsqrt(mean_sq + EPS) * gain).astype(BF16)


def attention_kernel(x_ref, gain_ref, wq_ref, wk_ref, wv_ref, o_ref, n_s, q_s, k_s, v_s, w_s):
    frames, features = x_ref.shape
    head_dim = features // HEADS
    n_s[...] = rms(x_ref[...].astype(F32), gain_ref[...])
    q_s[...] = (nn(n_s[...], wq_ref[...]) * (head_dim ** (-0.5) * LOG2E)).astype(BF16)
    k_s[...] = nn(n_s[...], wk_ref[...]).astype(BF16)
    v_s[...] = nn(n_s[...], wv_ref[...]).astype(BF16)
    half = frames // 2
    row = lax.broadcasted_iota(jnp.int32, (half, half), 0)
    col = lax.broadcasted_iota(jnp.int32, (half, half), 1)
    causal = row >= col
    low = lax.broadcasted_iota(jnp.int32, (1, 128), 1) < head_dim
    w_s[:half, half:] = jnp.zeros((half, half), BF16)
    for pair in range(features // 128):
        lanes = slice(pair * 128, pair * 128 + 128)
        mixed = []
        for mine in (low, jnp.logical_not(low)):
            q = jnp.where(mine, q_s[:, lanes], jnp.zeros((), BF16))
            t = nt(q, k_s[:, lanes])
            first = jnp.where(causal, t[:half, :half], MASKED)
            w = jnp.exp2(first - jnp.max(first, axis=1, keepdims=True))
            w_s[:half, :half] = w.astype(BF16)
            before = t[half:, :half]
            last = jnp.where(causal, t[half:, half:], MASKED)
            largest = jnp.maximum(
                jnp.max(before, axis=1, keepdims=True), jnp.max(last, axis=1, keepdims=True)
            )
            w_s[half:, :half] = jnp.exp2(before - largest).astype(BF16)
            w_s[half:, half:] = jnp.exp2(last - largest).astype(BF16)
            v = jnp.where(mine, v_s[:, lanes], jnp.ones((), BF16))
            mixed.append(nn(w_s[...], v))
        total = pltpu.roll(jnp.where(low, mixed[1], mixed[0]), head_dim, 1)
        o_ref[:, lanes] = (jnp.where(low, mixed[0], mixed[1]) / total).astype(BF16)


def residual_kernel(mixed_ref, x_ref, wo_ref, gain_ref, r_ref, m_ref):
    r = (x_ref[...].astype(F32) + nn(mixed_ref[...], wo_ref[...])).astype(BF16)
    r_ref[...] = r
    m_ref[...] = rms(r.astype(F32), gain_ref[...])


def keys_kernel(frames, positions, keys_ref, r_ref, m_ref, slots_ref, r_out, m_out):
    order = one_hot(frames * positions, frames, positions)
    r_out[...] = nn(order, r_ref[...]).astype(BF16)
    m_out[...] = nn(order, m_ref[...]).astype(BF16)
    half = SLOTS // 2
    core = lax.rem(lax.axis_index("pos"), 2)
    row = lax.broadcasted_iota(jnp.int32, (128, 256), 0)
    col = lax.broadcasted_iota(jnp.int32, (128, 256), 1)
    first = (row // half) * SLOTS + (row & (half - 1))
    count = keys_ref.shape[1] // 2
    for turn in range(2):
        taken = core if turn == 0 else 1 - core
        pick = jnp.where(col == first + taken * half, 1.0, 0.0).astype(BF16)
        for k in range(count // 128):
            keys = nt(pick, keys_ref[:, 256 * k : 256 * k + 256]).astype(BF16)
            for i in range(128 // half):
                at = turn * count + half * ORDER.index(k * (128 // half) + i)
                slots_ref[at : at + half, :] = keys[i * half : (i + 1) * half, :]


def combine_kernel(m_ref, slots_ref, c_ref):
    rows = 256
    for start in range(0, m_ref.shape[0], rows):
        part = slice(start, start + rows)
        t = nt(m_ref[part, :], slots_ref[...]) * (LOGIT_SCALE * LOG2E)
        w = jnp.exp2(t - jnp.max(t, axis=1, keepdims=True))
        c_ref[part, :] = (w / jnp.sum(w, axis=1, keepdims=True)).astype(BF16)


def dispatch_kernel(m_ref, other_ref, keys_ref, o_ref, all_s):
    tokens, features = m_ref.shape
    all_s[:tokens, :] = m_ref[...]
    all_s[tokens:, :] = other_ref[...]
    half = SLOTS // 2
    rows = 256
    for start in range(0, keys_ref.shape[0] // 2, rows):
        t = nt(keys_ref[start : start + rows, :], all_s[...]) * (LOGIT_SCALE * LOG2E)
        largest = jnp.max(t, axis=1, keepdims=True)
        w = jnp.exp2(t - largest)
        total = jnp.sum(w, axis=1, keepdims=True)
        sums = (nn(w.astype(BF16), all_s[...]) / total).astype(BF16)
        for k in range(rows // half):
            expert = start // half + k
            for j in range(features // 128):
                o_ref[expert, j * half : (j + 1) * half, :] = sums[
                    k * half : (k + 1) * half, j * 128 : (j + 1) * 128
                ]
        column = largest + jnp.log2(total)
        for at in range(0, rows, 128):
            lse = jnp.broadcast_to(column[at : at + 128], (128, 128)).T[:STAT_ROWS, :]
            high = lse.astype(BF16).astype(F32)
            middle = (lse - high).astype(BF16).astype(F32)
            rest = lse - high - middle
            line = lax.broadcasted_iota(jnp.int32, lse.shape, 0)
            stats = jnp.where(
                line == 0, high, jnp.where(line == 1, middle, jnp.where(line == 2, rest, 0.0))
            ).astype(BF16)
            for k in range(128 // half):
                o_ref[(start + at) // half + k, features // 128 * half :, :] = stats


def expert_kernel(got_ref, w_in_ref, other_in_ref, w_out_ref, other_out_ref, o_ref, w_s):
    chips, half, features = o_ref.shape
    tall = features // 128 * half
    lse = jnp.concatenate(
        [
            jnp.sum(got_ref[s, tall:, :].astype(F32), axis=0, keepdims=True)
            for s in range(chips)
        ],
        axis=0,
    )
    w = jnp.exp2(lse - jnp.max(lse, axis=0, keepdims=True))
    w = w / jnp.sum(w, axis=0, keepdims=True)
    w_s[...] = jnp.concatenate([w, jnp.zeros((128 - chips, 128), F32)], axis=0).T
    chip = lax.axis_index("pos") // 2
    place = sum(jnp.where(chip == ORDER[k], k, 0) for k in range(chips))
    place = lax.rem(place, 128 // half)
    mine = w_s[pl.ds(pl.multiple_of(place * half, half), half), :]
    columns = []
    for j in range(features // 128):
        total = jnp.zeros((half, 128), F32)
        for s in range(chips):
            total += mine[:, s : s + 1] * got_ref[s, j * half : (j + 1) * half, :].astype(F32)
        columns.append(total.astype(BF16))
    slot_in = jnp.concatenate(columns, axis=1)
    out = jnp.zeros((half, features), F32)
    for first, second in ((w_in_ref, w_out_ref), (other_in_ref, other_out_ref)):
        hidden = jax.nn.gelu(nn(slot_in, first[...])).astype(BF16)
        out += nn(hidden, second[...]).astype(BF16).astype(F32)
    out = out.astype(BF16)
    for s in range(chips):
        o_ref[s] = out


def own_kernel(r_ref, c_ref, own_ref, o_ref):
    count = own_ref.shape[0]
    o_ref[...] = r_ref[...].astype(F32) + nn(c_ref[:, :count], own_ref[...])


def output_kernel(sum_ref, c_ref, other_ref, o_ref):
    count = other_ref.shape[0]
    o_ref[...] = (sum_ref[...] + nn(c_ref[:, count:], other_ref[...])).astype(BF16)


def from_other_core(block):
    return lax.ppermute(block, "pos", [(k, k ^ 1) for k in range(lax.axis_size("pos"))])


def local(
    frames_in, attn_gain, w_query, w_key, w_value, w_output, moe_gain, dispatch_keys, w_in, w_out
):
    frame_count, pos_count, features = frames_in.shape
    tokens = frame_count * pos_count
    chips = lax.axis_size("pos") // 2
    half = SLOTS // 2
    by_core = [[2 * chip + core for chip in ORDER] for core in range(2)]
    wide = jax.ShapeDtypeStruct((tokens, features), BF16)

    def by_position(*refs):
        by_position_kernel(frame_count, pos_count, *refs)

    def keys(*refs):
        keys_kernel(frame_count, pos_count, *refs)

    def over_frames(block):
        block = block.reshape(pos_count, frame_count, features)
        block = lax.all_to_all(block, "frame", split_axis=0, concat_axis=0, tiled=True)
        return block.reshape(tokens, features)

    def over_chips(blocks):
        return lax.all_to_all(
            blocks, "pos", split_axis=0, concat_axis=0, tiled=True, axis_index_groups=by_core
        )

    other_in = from_other_core(w_in[0])
    other_out = from_other_core(w_out[0])
    line = jax.ShapeDtypeStruct((1, features), F32)
    x, gain, gain_moe = call(
        by_position,
        (wide, line, line),
        (frames_in.reshape(tokens, features), attn_gain.reshape(1, -1), moe_gain.reshape(1, -1)),
        flops=2 * tokens**2 * features,
    )
    spread = over_frames(x)
    mixed = call(
        attention_kernel,
        wide,
        (spread, gain, w_query, w_key, w_value),
        scratch=[pltpu.VMEM((tokens, features), BF16)] * 4 + [pltpu.VMEM((tokens, tokens), BF16)],
        flops=14 * tokens**2 * features,
        transcendentals=HEADS * tokens**2,
    )
    mixed = over_frames(mixed)
    residual, moe_input = call(
        residual_kernel,
        (wide, wide),
        (mixed, x, w_output, gain_moe),
        flops=2 * tokens**2 * features,
    )
    other_input = from_other_core(moe_input)
    slot_keys, residual, ordered_input = call(
        keys,
        (jax.ShapeDtypeStruct((EXPERTS * SLOTS, features), BF16), wide, wide),
        (dispatch_keys, residual, moe_input),
        flops=512 * tokens * features + 4 * tokens**2 * features,
    )
    sums = call(
        dispatch_kernel,
        jax.ShapeDtypeStruct((chips, features // 128 * half + STAT_ROWS, 128), BF16),
        (moe_input, other_input, slot_keys),
        scratch=[pltpu.VMEM((2 * tokens, features), BF16)],
        flops=8 * tokens**2 * features,
        transcendentals=2 * tokens**2,
    )
    outputs = call(
        expert_kernel,
        jax.ShapeDtypeStruct((chips, half, features), BF16),
        (over_chips(sums), w_in[0], other_in, w_out[0], other_out),
        scratch=[pltpu.VMEM((128, 128), F32)],
        flops=16 * SLOTS * features**2,
    )
    own_half = over_chips(outputs).reshape(-1, features)
    other_half = from_other_core(own_half)
    combine = call(
        combine_kernel,
        jax.ShapeDtypeStruct((tokens, EXPERTS * SLOTS), BF16),
        (ordered_input, slot_keys),
        flops=4 * tokens**2 * features,
        transcendentals=2 * tokens**2,
    )
    own_sum = call(
        own_kernel,
        jax.ShapeDtypeStruct((tokens, features), F32),
        (residual, combine, own_half),
        flops=2 * tokens**2 * features,
    )
    out = call(
        output_kernel, wide, (own_sum, combine, other_half), flops=2 * tokens**2 * features
    )
    return out.reshape(frame_count, pos_count, features)


def solution(mesh):
    in_specs = (
        P("frame", "pos", None),
        P(),
        P(),
        P(),
        P(),
        P(),
        P(),
        P(),
        P("pos", None, None),
        P("pos", None, None),
    )
    out_specs = P("frame", "pos", None)

    return jax.shard_map(local, mesh=mesh, in_specs=in_specs, out_specs=out_specs, check_vma=False)
```

```python
import jax
import jax.numpy as jnp
from jax import lax
from jax.experimental import pallas as pl
from jax.experimental.pallas import tpu as pltpu
from jax.sharding import PartitionSpec as P


HEADS = 8
EXPERTS = 16
SLOTS = 64

EPS = 1e-06
LOGIT_SCALE = 3.0
MASKED = -1e30
LOG2E = 1.4426950408889634

F32 = jnp.float32
BF16 = jnp.bfloat16
VMEM = pl.BlockSpec(memory_space=pltpu.VMEM)
STAT_ROWS = 8
ORDER = (9, 11, 13, 15, 1, 3, 5, 7, 8, 10, 12, 14, 0, 2, 4, 6)
BACK = ORDER
FRAMES = (5, 7, 4, 6, 3, 2, 1, 0)


def nn(a, b):
    return lax.dot_general(a, b, (((1,), (0,)), ((), ())), preferred_element_type=F32)


def nt(a, b):
    return lax.dot_general(a, b, (((1,), (1,)), ((), ())), preferred_element_type=F32)


def call(kernel, out_shape, args, scratch=(), flops=1 << 20, transcendentals=0):
    single = isinstance(out_shape, jax.ShapeDtypeStruct)
    outs = (out_shape,) if single else tuple(out_shape)
    moved = sum(a.size * a.dtype.itemsize for a in (*args, *outs))
    return pl.pallas_call(
        kernel,
        out_shape=out_shape,
        in_specs=[VMEM] * len(args),
        out_specs=VMEM if single else tuple([VMEM] * len(outs)),
        scratch_shapes=list(scratch),
        compiler_params=pltpu.CompilerParams(vmem_limit_bytes=16 << 20),
        cost_estimate=pl.CostEstimate(
            flops=flops, bytes_accessed=moved, transcendentals=transcendentals
        ),
    )(*args)


def one_hot(rows, outer, inner):
    row = lax.broadcasted_iota(jnp.int32, (rows, rows), 0)
    col = lax.broadcasted_iota(jnp.int32, (rows, rows), 1)
    source = (row & (inner - 1)) * outer + lax.shift_right_logical(row, inner.bit_length() - 1)
    return jnp.where(col == source, 1.0, 0.0).astype(BF16)


def by_position_kernel(frames, positions, x_ref, gain_ref, moe_ref, o_ref, gain_out, moe_out):
    gain_out[...] = gain_ref[...]
    moe_out[...] = moe_ref[...]
    o_ref[...] = nn(one_hot(frames * positions, positions, frames), x_ref[...]).astype(BF16)


def rms(rows, gain):
    mean_sq = jnp.mean(rows * rows, axis=-1, keepdims=True)
    return (rows * lax.rsqrt(mean_sq + EPS) * gain).astype(BF16)


def attention_kernel(x_ref, gain_ref, wq_ref, wk_ref, wv_ref, o_ref, n_s, q_s, k_s, v_s, w_s):
    frames, features = x_ref.shape
    head_dim = features // HEADS
    run = frames // len(FRAMES)
    for i, place in enumerate(FRAMES):
        n_s[place * run : (place + 1) * run, :] = rms(
            x_ref[i * run : (i + 1) * run, :].astype(F32), gain_ref[...]
        )
    q_s[...] = (nn(n_s[...], wq_ref[...]) * (head_dim ** (-0.5) * LOG2E)).astype(BF16)
    k_s[...] = nn(n_s[...], wk_ref[...]).astype(BF16)
    v_s[...] = nn(n_s[...], wv_ref[...]).astype(BF16)
    half = frames // 2
    row = lax.broadcasted_iota(jnp.int32, (half, half), 0)
    col = lax.broadcasted_iota(jnp.int32, (half, half), 1)
    causal = row >= col
    low = lax.broadcasted_iota(jnp.int32, (1, 128), 1) < head_dim
    w_s[:half, half:] = jnp.zeros((half, half), BF16)
    for pair in range(features // 128):
        lanes = slice(pair * 128, pair * 128 + 128)
        mixed = []
        for mine in (low, jnp.logical_not(low)):
            q = jnp.where(mine, q_s[:, lanes], jnp.zeros((), BF16))
            t = nt(q, k_s[:, lanes])
            first = jnp.where(causal, t[:half, :half], MASKED)
            w = jnp.exp2(first - jnp.max(first, axis=1, keepdims=True))
            w_s[:half, :half] = w.astype(BF16)
            before = t[half:, :half]
            last = jnp.where(causal, t[half:, half:], MASKED)
            largest = jnp.maximum(
                jnp.max(before, axis=1, keepdims=True), jnp.max(last, axis=1, keepdims=True)
            )
            w_s[half:, :half] = jnp.exp2(before - largest).astype(BF16)
            w_s[half:, half:] = jnp.exp2(last - largest).astype(BF16)
            v = jnp.where(mine, v_s[:, lanes], jnp.ones((), BF16))
            mixed.append(nn(w_s[...], v))
        total = pltpu.roll(jnp.where(low, mixed[1], mixed[0]), head_dim, 1)
        out = (jnp.where(low, mixed[0], mixed[1]) / total).astype(BF16)
        for i, place in enumerate(FRAMES):
            o_ref[i * run : (i + 1) * run, lanes] = out[place * run : (place + 1) * run, :]


def residual_kernel(mixed_ref, x_ref, wo_ref, gain_ref, r_ref, m_ref):
    r = (x_ref[...].astype(F32) + nn(mixed_ref[...], wo_ref[...])).astype(BF16)
    r_ref[...] = r
    m_ref[...] = rms(r.astype(F32), gain_ref[...])


def keys_kernel(frames, positions, keys_ref, r_ref, m_ref, own_ref, slots_ref, r_out, m_out):
    order = one_hot(frames * positions, frames, positions)
    r_out[...] = nn(order, r_ref[...]).astype(BF16)
    m_out[...] = nn(order, m_ref[...]).astype(BF16)
    half = SLOTS // 2
    core = lax.rem(lax.axis_index("pos"), 2)
    row = lax.broadcasted_iota(jnp.int32, (128, 256), 0)
    col = lax.broadcasted_iota(jnp.int32, (128, 256), 1)
    first = (row // half) * SLOTS + (row & (half - 1))
    count = keys_ref.shape[1] // 2
    for turn in range(2):
        taken = core if turn == 0 else 1 - core
        pick = jnp.where(col == first + taken * half, 1.0, 0.0).astype(BF16)
        for k in range(count // 128):
            keys = nt(pick, keys_ref[:, 256 * k : 256 * k + 256]).astype(BF16)
            for i in range(128 // half):
                chip = k * (128 // half) + i
                rows = keys[i * half : (i + 1) * half, :]
                at = turn * count + half * BACK.index(chip)
                slots_ref[at : at + half, :] = rows
                if turn == 0:
                    at = half * ORDER.index(chip)
                    own_ref[at : at + half, :] = rows


def combine_kernel(m_ref, slots_ref, c_ref):
    rows = 256
    for start in range(0, m_ref.shape[0], rows):
        part = slice(start, start + rows)
        t = nt(m_ref[part, :], slots_ref[...]) * (LOGIT_SCALE * LOG2E)
        w = jnp.exp2(t - jnp.max(t, axis=1, keepdims=True))
        c_ref[part, :] = (w / jnp.sum(w, axis=1, keepdims=True)).astype(BF16)


def dispatch_kernel(m_ref, other_ref, keys_ref, o_ref, all_s):
    tokens, features = m_ref.shape
    all_s[:tokens, :] = m_ref[...]
    all_s[tokens:, :] = other_ref[...]
    half = SLOTS // 2
    rows = 256
    for start in range(0, keys_ref.shape[0], rows):
        t = nt(keys_ref[start : start + rows, :], all_s[...]) * (LOGIT_SCALE * LOG2E)
        largest = jnp.max(t, axis=1, keepdims=True)
        w = jnp.exp2(t - largest)
        total = jnp.sum(w, axis=1, keepdims=True)
        sums = (nn(w.astype(BF16), all_s[...]) / total).astype(BF16)
        for k in range(rows // half):
            expert = start // half + k
            for j in range(features // 128):
                o_ref[expert, j * half : (j + 1) * half, :] = sums[
                    k * half : (k + 1) * half, j * 128 : (j + 1) * 128
                ]
        column = largest + jnp.log2(total)
        for at in range(0, rows, 128):
            lse = jnp.broadcast_to(column[at : at + 128], (128, 128)).T[:STAT_ROWS, :]
            high = lse.astype(BF16).astype(F32)
            middle = (lse - high).astype(BF16).astype(F32)
            rest = lse - high - middle
            line = lax.broadcasted_iota(jnp.int32, lse.shape, 0)
            stats = jnp.where(
                line == 0, high, jnp.where(line == 1, middle, jnp.where(line == 2, rest, 0.0))
            ).astype(BF16)
            for k in range(128 // half):
                o_ref[(start + at) // half + k, features // 128 * half :, :] = stats


def expert_kernel(got_ref, w_in_ref, other_in_ref, w_out_ref, other_out_ref, o_ref, w_s):
    chips, half, features = o_ref.shape
    tall = features // 128 * half
    lse = jnp.concatenate(
        [
            jnp.sum(got_ref[s, tall:, :].astype(F32), axis=0, keepdims=True)
            for s in range(chips)
        ],
        axis=0,
    )
    w = jnp.exp2(lse - jnp.max(lse, axis=0, keepdims=True))
    w = w / jnp.sum(w, axis=0, keepdims=True)
    w_s[...] = jnp.concatenate([w, jnp.zeros((128 - chips, 128), F32)], axis=0).T
    chip = lax.axis_index("pos") // 2
    place = sum(jnp.where(chip == ORDER[k], k, 0) for k in range(chips))
    place = lax.rem(place, 128 // half)
    mine = w_s[pl.ds(pl.multiple_of(place * half, half), half), :]
    columns = []
    for j in range(features // 128):
        total = jnp.zeros((half, 128), F32)
        for s in range(chips):
            total += mine[:, s : s + 1] * got_ref[s, j * half : (j + 1) * half, :].astype(F32)
        columns.append(total.astype(BF16))
    slot_in = jnp.concatenate(columns, axis=1)
    out = jnp.zeros((half, features), F32)
    for first, second in ((w_in_ref, w_out_ref), (other_in_ref, other_out_ref)):
        hidden = jax.nn.gelu(nn(slot_in, first[...])).astype(BF16)
        out += nn(hidden, second[...]).astype(BF16).astype(F32)
    out = out.astype(BF16)
    for s in range(chips):
        o_ref[s] = out


def own_kernel(r_ref, c_ref, own_ref, o_ref):
    count = own_ref.shape[0]
    o_ref[...] = r_ref[...].astype(F32) + nn(c_ref[:, :count], own_ref[...])


def output_kernel(sum_ref, c_ref, other_ref, o_ref):
    count = other_ref.shape[0]
    o_ref[...] = (sum_ref[...] + nn(c_ref[:, count:], other_ref[...])).astype(BF16)


def from_other_core(block):
    return lax.ppermute(block, "pos", [(k, k ^ 1) for k in range(lax.axis_size("pos"))])


def local(
    frames_in, attn_gain, w_query, w_key, w_value, w_output, moe_gain, dispatch_keys, w_in, w_out
):
    frame_count, pos_count, features = frames_in.shape
    tokens = frame_count * pos_count
    chips = lax.axis_size("pos") // 2
    half = SLOTS // 2
    wide = jax.ShapeDtypeStruct((tokens, features), BF16)

    def by_position(*refs):
        by_position_kernel(frame_count, pos_count, *refs)

    def keys(*refs):
        keys_kernel(frame_count, pos_count, *refs)

    def over_frames(block):
        block = block.reshape(pos_count, frame_count, features)
        block = lax.all_to_all(
            block, "frame", split_axis=0, concat_axis=0, tiled=True, axis_index_groups=[list(FRAMES)]
        )
        return block.reshape(tokens, features)

    def over_chips(blocks, order):
        by_core = [[2 * chip + core for chip in order] for core in range(2)]
        return lax.all_to_all(
            blocks, "pos", split_axis=0, concat_axis=0, tiled=True, axis_index_groups=by_core
        )

    other_in = from_other_core(w_in[0])
    other_out = from_other_core(w_out[0])
    line = jax.ShapeDtypeStruct((1, features), F32)
    x, gain, gain_moe = call(
        by_position,
        (wide, line, line),
        (frames_in.reshape(tokens, features), attn_gain.reshape(1, -1), moe_gain.reshape(1, -1)),
        flops=2 * tokens**2 * features,
    )
    spread = over_frames(x)
    mixed = call(
        attention_kernel,
        wide,
        (spread, gain, w_query, w_key, w_value),
        scratch=[pltpu.VMEM((tokens, features), BF16)] * 4 + [pltpu.VMEM((tokens, tokens), BF16)],
        flops=14 * tokens**2 * features,
        transcendentals=HEADS * tokens**2,
    )
    mixed = over_frames(mixed)
    residual, moe_input = call(
        residual_kernel,
        (wide, wide),
        (mixed, x, w_output, gain_moe),
        flops=2 * tokens**2 * features,
    )
    other_input = from_other_core(moe_input)
    own_keys, slot_keys, residual, ordered_input = call(
        keys,
        (
            jax.ShapeDtypeStruct((chips * half, features), BF16),
            jax.ShapeDtypeStruct((2 * chips * half, features), BF16),
            wide,
            wide,
        ),
        (dispatch_keys, residual, moe_input),
        flops=512 * tokens * features + 4 * tokens**2 * features,
    )
    sums = call(
        dispatch_kernel,
        jax.ShapeDtypeStruct((chips, features // 128 * half + STAT_ROWS, 128), BF16),
        (moe_input, other_input, own_keys),
        scratch=[pltpu.VMEM((2 * tokens, features), BF16)],
        flops=8 * tokens**2 * features,
        transcendentals=2 * tokens**2,
    )
    outputs = call(
        expert_kernel,
        jax.ShapeDtypeStruct((chips, half, features), BF16),
        (over_chips(sums, ORDER), w_in[0], other_in, w_out[0], other_out),
        scratch=[pltpu.VMEM((128, 128), F32)],
        flops=16 * SLOTS * features**2,
    )
    own_half = over_chips(outputs, BACK).reshape(-1, features)
    other_half = from_other_core(own_half)
    combine = call(
        combine_kernel,
        jax.ShapeDtypeStruct((tokens, EXPERTS * SLOTS), BF16),
        (ordered_input, slot_keys),
        flops=4 * tokens**2 * features,
        transcendentals=2 * tokens**2,
    )
    own_sum = call(
        own_kernel,
        jax.ShapeDtypeStruct((tokens, features), F32),
        (residual, combine, own_half),
        flops=2 * tokens**2 * features,
    )
    out = call(
        output_kernel, wide, (own_sum, combine, other_half), flops=2 * tokens**2 * features
    )
    return out.reshape(frame_count, pos_count, features)


def solution(mesh):
    in_specs = (
        P("frame", "pos", None),
        P(),
        P(),
        P(),
        P(),
        P(),
        P(),
        P(),
        P("pos", None, None),
        P("pos", None, None),
    )
    out_specs = P("frame", "pos", None)

    return jax.shard_map(local, mesh=mesh, in_specs=in_specs, out_specs=out_specs, check_vma=False)
```

```python
import jax
import jax.numpy as jnp
from jax import lax
from jax.experimental import pallas as pl
from jax.experimental.pallas import tpu as pltpu
from jax.sharding import PartitionSpec as P


HEADS = 8
EXPERTS = 16
SLOTS = 64

EPS = 1e-06
LOGIT_SCALE = 3.0
MASKED = -1e30
LOG2E = 1.4426950408889634

F32 = jnp.float32
BF16 = jnp.bfloat16
VMEM = pl.BlockSpec(memory_space=pltpu.VMEM)
STAT_ROWS = 8
ORDER = (9, 11, 13, 15, 1, 3, 5, 7, 8, 10, 12, 14, 0, 2, 4, 6)
BACK = ORDER
FRAMES = (5, 7, 4, 6, 3, 2, 1, 0)


def nn(a, b):
    return lax.dot_general(a, b, (((1,), (0,)), ((), ())), preferred_element_type=F32)


def nt(a, b):
    return lax.dot_general(a, b, (((1,), (1,)), ((), ())), preferred_element_type=F32)


def call(kernel, out_shape, args, scratch=(), flops=1 << 20, transcendentals=0, out_left=False):
    single = isinstance(out_shape, jax.ShapeDtypeStruct)
    outs = (out_shape,) if single else tuple(out_shape)
    moved = sum(a.size * a.dtype.itemsize for a in (*args, *outs))
    return pl.pallas_call(
        kernel,
        out_shape=out_shape,
        in_specs=[VMEM] * len(args),
        out_specs=(pl.BlockSpec(memory_space=pl.ANY) if out_left else VMEM)
        if single
        else tuple([VMEM] * len(outs)),
        scratch_shapes=list(scratch),
        compiler_params=pltpu.CompilerParams(vmem_limit_bytes=16 << 20),
        cost_estimate=pl.CostEstimate(
            flops=flops, bytes_accessed=moved, transcendentals=transcendentals
        ),
    )(*args)


def one_hot(rows, outer, inner):
    row = lax.broadcasted_iota(jnp.int32, (rows, rows), 0)
    col = lax.broadcasted_iota(jnp.int32, (rows, rows), 1)
    source = (row & (inner - 1)) * outer + lax.shift_right_logical(row, inner.bit_length() - 1)
    return jnp.where(col == source, 1.0, 0.0).astype(BF16)


def by_position_kernel(frames, positions, x_ref, gain_ref, moe_ref, o_ref, gain_out, moe_out):
    gain_out[...] = gain_ref[...]
    moe_out[...] = moe_ref[...]
    o_ref[...] = nn(one_hot(frames * positions, positions, frames), x_ref[...]).astype(BF16)


def rms(rows, gain):
    mean_sq = jnp.mean(rows * rows, axis=-1, keepdims=True)
    return (rows * lax.rsqrt(mean_sq + EPS) * gain).astype(BF16)


def attention_kernel(x_ref, gain_ref, wq_ref, wk_ref, wv_ref, o_ref, n_s, q_s, k_s, v_s, w_s):
    frames, features = x_ref.shape
    head_dim = features // HEADS
    run = frames // len(FRAMES)
    for i, place in enumerate(FRAMES):
        n_s[place * run : (place + 1) * run, :] = rms(
            x_ref[i * run : (i + 1) * run, :].astype(F32), gain_ref[...]
        )
    q_s[...] = (nn(n_s[...], wq_ref[...]) * (head_dim ** (-0.5) * LOG2E)).astype(BF16)
    k_s[...] = nn(n_s[...], wk_ref[...]).astype(BF16)
    v_s[...] = nn(n_s[...], wv_ref[...]).astype(BF16)
    half = frames // 2
    row = lax.broadcasted_iota(jnp.int32, (half, half), 0)
    col = lax.broadcasted_iota(jnp.int32, (half, half), 1)
    causal = row >= col
    low = lax.broadcasted_iota(jnp.int32, (1, 128), 1) < head_dim
    w_s[:half, half:] = jnp.zeros((half, half), BF16)
    for pair in range(features // 128):
        lanes = slice(pair * 128, pair * 128 + 128)
        mixed = []
        for mine in (low, jnp.logical_not(low)):
            q = jnp.where(mine, q_s[:, lanes], jnp.zeros((), BF16))
            t = nt(q, k_s[:, lanes])
            first = jnp.where(causal, t[:half, :half], MASKED)
            w = jnp.exp2(first - jnp.max(first, axis=1, keepdims=True))
            w_s[:half, :half] = w.astype(BF16)
            before = t[half:, :half]
            last = jnp.where(causal, t[half:, half:], MASKED)
            largest = jnp.maximum(
                jnp.max(before, axis=1, keepdims=True), jnp.max(last, axis=1, keepdims=True)
            )
            w_s[half:, :half] = jnp.exp2(before - largest).astype(BF16)
            w_s[half:, half:] = jnp.exp2(last - largest).astype(BF16)
            v = jnp.where(mine, v_s[:, lanes], jnp.ones((), BF16))
            mixed.append(nn(w_s[...], v))
        total = pltpu.roll(jnp.where(low, mixed[1], mixed[0]), head_dim, 1)
        out = (jnp.where(low, mixed[0], mixed[1]) / total).astype(BF16)
        for i, place in enumerate(FRAMES):
            o_ref[i * run : (i + 1) * run, lanes] = out[place * run : (place + 1) * run, :]


def residual_kernel(mixed_ref, x_ref, wo_ref, gain_ref, r_ref, m_ref):
    r = (x_ref[...].astype(F32) + nn(mixed_ref[...], wo_ref[...])).astype(BF16)
    r_ref[...] = r
    m_ref[...] = rms(r.astype(F32), gain_ref[...])


def keys_kernel(frames, positions, keys_ref, r_ref, m_ref, own_ref, slots_ref, r_out, m_out):
    order = one_hot(frames * positions, frames, positions)
    r_out[...] = nn(order, r_ref[...]).astype(BF16)
    m_out[...] = nn(order, m_ref[...]).astype(BF16)
    half = SLOTS // 2
    core = lax.rem(lax.axis_index("pos"), 2)
    row = lax.broadcasted_iota(jnp.int32, (128, 256), 0)
    col = lax.broadcasted_iota(jnp.int32, (128, 256), 1)
    first = (row // half) * SLOTS + (row & (half - 1))
    count = keys_ref.shape[1] // 2
    for turn in range(2):
        taken = core if turn == 0 else 1 - core
        pick = jnp.where(col == first + taken * half, 1.0, 0.0).astype(BF16)
        for k in range(count // 128):
            keys = nt(pick, keys_ref[:, 256 * k : 256 * k + 256]).astype(BF16)
            for i in range(128 // half):
                chip = k * (128 // half) + i
                rows = keys[i * half : (i + 1) * half, :]
                at = turn * count + half * BACK.index(chip)
                slots_ref[at : at + half, :] = rows
                if turn == 0:
                    at = half * ORDER.index(chip)
                    own_ref[at : at + half, :] = rows


def combine_kernel(m_ref, slots_ref, c_ref):
    rows = 256
    for start in range(0, m_ref.shape[0], rows):
        part = slice(start, start + rows)
        t = nt(m_ref[part, :], slots_ref[...]) * (LOGIT_SCALE * LOG2E)
        w = jnp.exp2(t - jnp.max(t, axis=1, keepdims=True))
        c_ref[part, :] = (w / jnp.sum(w, axis=1, keepdims=True)).astype(BF16)


def dispatch_kernel(m_ref, other_ref, keys_ref, o_ref, all_s):
    tokens, features = m_ref.shape
    all_s[:tokens, :] = m_ref[...]
    all_s[tokens:, :] = other_ref[...]
    half = SLOTS // 2
    rows = 512
    for start in range(0, keys_ref.shape[0], rows):
        t = nt(keys_ref[start : start + rows, :], all_s[...]) * (LOGIT_SCALE * LOG2E)
        largest = jnp.max(t, axis=1, keepdims=True)
        w = jnp.exp2(t - largest)
        total = jnp.sum(w, axis=1, keepdims=True)
        sums = (nn(w.astype(BF16), all_s[...]) / total).astype(BF16)
        for k in range(rows // half):
            expert = start // half + k
            for j in range(features // 128):
                o_ref[expert, j * half : (j + 1) * half, :] = sums[
                    k * half : (k + 1) * half, j * 128 : (j + 1) * 128
                ]
        column = largest + jnp.log2(total)
        for at in range(0, rows, 128):
            lse = jnp.broadcast_to(column[at : at + 128], (128, 128)).T[:STAT_ROWS, :]
            high = lse.astype(BF16).astype(F32)
            middle = (lse - high).astype(BF16).astype(F32)
            rest = lse - high - middle
            line = lax.broadcasted_iota(jnp.int32, lse.shape, 0)
            stats = jnp.where(
                line == 0, high, jnp.where(line == 1, middle, jnp.where(line == 2, rest, 0.0))
            ).astype(BF16)
            for k in range(128 // half):
                o_ref[(start + at) // half + k, features // 128 * half :, :] = stats


def expert_kernel(got_ref, w_in_ref, other_in_ref, w_out_ref, other_out_ref, o_ref, w_s):
    chips, half, features = o_ref.shape
    tall = features // 128 * half
    lse = jnp.concatenate(
        [
            jnp.sum(got_ref[s, tall:, :].astype(F32), axis=0, keepdims=True)
            for s in range(chips)
        ],
        axis=0,
    )
    w = jnp.exp2(lse - jnp.max(lse, axis=0, keepdims=True))
    w = w / jnp.sum(w, axis=0, keepdims=True)
    w_s[...] = jnp.concatenate([w, jnp.zeros((128 - chips, 128), F32)], axis=0).T
    chip = lax.axis_index("pos") // 2
    place = sum(jnp.where(chip == ORDER[k], k, 0) for k in range(chips))
    place = lax.rem(place, 128 // half)
    mine = w_s[pl.ds(pl.multiple_of(place * half, half), half), :]
    columns = []
    for j in range(features // 128):
        total = jnp.zeros((half, 128), F32)
        for s in range(chips):
            total += mine[:, s : s + 1] * got_ref[s, j * half : (j + 1) * half, :].astype(F32)
        columns.append(total.astype(BF16))
    slot_in = jnp.concatenate(columns, axis=1)
    out = jnp.zeros((half, features), F32)
    for first, second in ((w_in_ref, w_out_ref), (other_in_ref, other_out_ref)):
        hidden = jax.nn.gelu(nn(slot_in, first[...])).astype(BF16)
        out += nn(hidden, second[...]).astype(BF16).astype(F32)
    out = out.astype(BF16)
    for s in range(chips):
        o_ref[s] = out


def own_kernel(r_ref, c_ref, own_ref, o_ref):
    count = own_ref.shape[0]
    o_ref[...] = r_ref[...].astype(F32) + nn(c_ref[:, :count], own_ref[...])


def output_kernel(sum_ref, c_ref, other_ref, o_ref, rows_s, sems):
    count = other_ref.shape[0]
    run = sum_ref.shape[0] // 2
    copies = []
    for k in range(2):
        part = slice(k * run, (k + 1) * run)
        rows = sum_ref[part, :] + nn(c_ref[part, count:], other_ref[...])
        rows_s[part, :] = rows.astype(BF16)
        copies.append(pltpu.make_async_copy(rows_s.at[part, :], o_ref.at[part, :], sems.at[k]))
        copies[k].start()
    for copy in copies:
        copy.wait()


def from_other_core(block):
    return lax.ppermute(block, "pos", [(k, k ^ 1) for k in range(lax.axis_size("pos"))])


def local(
    frames_in, attn_gain, w_query, w_key, w_value, w_output, moe_gain, dispatch_keys, w_in, w_out
):
    frame_count, pos_count, features = frames_in.shape
    tokens = frame_count * pos_count
    chips = lax.axis_size("pos") // 2
    half = SLOTS // 2
    wide = jax.ShapeDtypeStruct((tokens, features), BF16)

    def by_position(*refs):
        by_position_kernel(frame_count, pos_count, *refs)

    def keys(*refs):
        keys_kernel(frame_count, pos_count, *refs)

    def over_frames(block):
        block = block.reshape(pos_count, frame_count, features)
        block = lax.all_to_all(
            block, "frame", split_axis=0, concat_axis=0, tiled=True, axis_index_groups=[list(FRAMES)]
        )
        return block.reshape(tokens, features)

    def over_chips(blocks, order):
        by_core = [[2 * chip + core for chip in order] for core in range(2)]
        return lax.all_to_all(
            blocks, "pos", split_axis=0, concat_axis=0, tiled=True, axis_index_groups=by_core
        )

    other_in = from_other_core(w_in[0])
    other_out = from_other_core(w_out[0])
    line = jax.ShapeDtypeStruct((1, features), F32)
    x, gain, gain_moe = call(
        by_position,
        (wide, line, line),
        (frames_in.reshape(tokens, features), attn_gain.reshape(1, -1), moe_gain.reshape(1, -1)),
        flops=2 * tokens**2 * features,
    )
    spread = over_frames(x)
    mixed = call(
        attention_kernel,
        wide,
        (spread, gain, w_query, w_key, w_value),
        scratch=[pltpu.VMEM((tokens, features), BF16)] * 4 + [pltpu.VMEM((tokens, tokens), BF16)],
        flops=14 * tokens**2 * features,
        transcendentals=HEADS * tokens**2,
    )
    mixed = over_frames(mixed)
    residual, moe_input = call(
        residual_kernel,
        (wide, wide),
        (mixed, x, w_output, gain_moe),
        flops=2 * tokens**2 * features,
    )
    other_input = from_other_core(moe_input)
    own_keys, slot_keys, residual, ordered_input = call(
        keys,
        (
            jax.ShapeDtypeStruct((chips * half, features), BF16),
            jax.ShapeDtypeStruct((2 * chips * half, features), BF16),
            wide,
            wide,
        ),
        (dispatch_keys, residual, moe_input),
        flops=512 * tokens * features + 4 * tokens**2 * features,
    )
    sums = call(
        dispatch_kernel,
        jax.ShapeDtypeStruct((chips, features // 128 * half + STAT_ROWS, 128), BF16),
        (moe_input, other_input, own_keys),
        scratch=[pltpu.VMEM((2 * tokens, features), BF16)],
        flops=8 * tokens**2 * features,
        transcendentals=2 * tokens**2,
    )
    outputs = call(
        expert_kernel,
        jax.ShapeDtypeStruct((chips, half, features), BF16),
        (over_chips(sums, ORDER), w_in[0], other_in, w_out[0], other_out),
        scratch=[pltpu.VMEM((128, 128), F32)],
        flops=16 * SLOTS * features**2,
    )
    own_half = over_chips(outputs, BACK).reshape(-1, features)
    other_half = from_other_core(own_half)
    combine = call(
        combine_kernel,
        jax.ShapeDtypeStruct((tokens, EXPERTS * SLOTS), BF16),
        (ordered_input, slot_keys),
        flops=4 * tokens**2 * features,
        transcendentals=2 * tokens**2,
    )
    own_sum = call(
        own_kernel,
        jax.ShapeDtypeStruct((tokens, features), F32),
        (residual, combine, own_half),
        flops=2 * tokens**2 * features,
    )
    out = call(
        output_kernel,
        wide,
        (own_sum, combine, other_half),
        scratch=[pltpu.VMEM((tokens, features), BF16), pltpu.SemaphoreType.DMA((2,))],
        flops=2 * tokens**2 * features,
        out_left=True,
    )
    return out.reshape(frame_count, pos_count, features)


def solution(mesh):
    in_specs = (
        P("frame", "pos", None),
        P(),
        P(),
        P(),
        P(),
        P(),
        P(),
        P(),
        P("pos", None, None),
        P("pos", None, None),
    )
    out_specs = P("frame", "pos", None)

    return jax.shard_map(local, mesh=mesh, in_specs=in_specs, out_specs=out_specs, check_vma=False)
```
